32 devices in a mesh: row: 4 (over y, x), col: 8 (over z, core).
Axes of the slice: x: 2, y: 2, z: 4, core: 2. Of those that a mesh axis runs over, the one named last changes fastest.
Arguments:
- x_slab: bfloat16 [8, 16, 64, 128], P('row', 'col'), may hold values from -220 to 220
- h_blocks: bfloat16 [8, 16, 25, 4096], P('row', 'col'), may hold values from -0.21875 to 0.21875
- h_cols: int32 [8, 16, 25], P('row', 'col'), may hold values from 0 to 127, as said below
- h_count: int32 [8, 16], P('row', 'col'), may hold values from 1 to 25, as said below
- z_blocks: bfloat16 [8, 16, 25, 4096], P('row', 'col'), may hold values from -0.15625 to 0.15625
- z_cols: int32 [8, 16, 25], P('row', 'col'), may hold values from 0 to 127, as said below
- z_count: int32 [8, 16], P('row', 'col'), may hold values from 1 to 25, as said below
Outputs:
- cheb_one: bfloat16 [8, 16, 64, 128], P('row', 'col')
- cheb_two: bfloat16 [8, 16, 64, 128], P('row', 'col')
The draws below stay inside these ranges and needn't reach their ends.
Inputs may be any that keep to these rules, and one draw needn't show every extreme that they name: `h_cols`: the 25 entries of a block cell name the 25 distinct cells within 2 cells of it along each lattice dimension, the lattice being periodic; only the first h_count entries of a cell are live, the others are padding. `h_count`: some cell has 25 live entries and some cell has 1. `z_cols`: the 25 entries of a block cell name the 25 distinct cells within 2 cells of it along each lattice dimension, the lattice being periodic; only the first z_count entries of a cell are live, the others are padding. `z_count`: some cell has 25 live entries and some cell has 1.
All inputs are finite; a program needn't handle non-finite values.
Results may differ from the reference program's by a relative error of at most 0.0085.
Values may be sent and summed in bfloat16 or wider, within the bound.
A program may use at most 64 MiB of HBM per device.

```python
import jax
import jax.numpy as jnp
from jax import lax

BLOCK = 64
SIDE = 2
SLAB = 128
REACH = 2
ENTRIES = 25
LAT_Y = 8
LAT_X = 16


def draw_x_slab(key, part):
    noise_key, row_key, col_key = jax.random.split(key, 3)
    values = jax.random.truncated_normal(noise_key, -4.0, 4.0, (LAT_Y, LAT_X, BLOCK, SLAB), jnp.float32)
    row_scale = jnp.exp(jax.random.uniform(row_key, (LAT_Y, LAT_X, BLOCK, 1), jnp.float32, -1.15, 1.15))
    col_scale = jnp.exp(jax.random.uniform(col_key, (1, 1, 1, SLAB), jnp.float32, -1.15, 1.15))
    lat_row = lax.broadcasted_iota(jnp.int32, (LAT_Y, LAT_X, 1, 1), 0)
    lat_col = lax.broadcasted_iota(jnp.int32, (LAT_Y, LAT_X, 1, 1), 1)
    domain_id = lat_row // SIDE * (LAT_X // SIDE) + lat_col // SIDE
    domain_total = LAT_Y // SIDE * (LAT_X // SIDE)
    position = domain_id.astype(jnp.float32) / max(domain_total - 1, 1)
    trend_scale = jnp.sqrt(1.0 + 2.0 * position)
    return (values * row_scale * col_scale * trend_scale).astype(jnp.bfloat16)


def entry_lists(key, salt):
    base_key = jax.random.fold_in(key, salt)
    cap_key, fill_key, full_key, spot_key, least_key, order_key = jax.random.split(base_key, 6)
    domain_total = LAT_Y // SIDE * (LAT_X // SIDE)
    domain_ids = jnp.arange(domain_total, dtype=jnp.int32)
    full_domain = jax.random.randint(full_key, (), 0, domain_total)
    domain_caps = jax.random.randint(cap_key, (domain_total,), ENTRIES // 3, ENTRIES + 1)
    domain_caps = jnp.where(domain_ids == full_domain, ENTRIES, domain_caps)
    lat_row = lax.broadcasted_iota(jnp.int32, (LAT_Y, LAT_X), 0)
    lat_col = lax.broadcasted_iota(jnp.int32, (LAT_Y, LAT_X), 1)
    domain_of = lat_row // SIDE * (LAT_X // SIDE) + lat_col // SIDE
    local_cell = lat_row % SIDE * SIDE + lat_col % SIDE
    cell_cap = domain_caps[domain_of]
    counts = jax.random.randint(fill_key, (LAT_Y, LAT_X), jnp.maximum(cell_cap // 2, 1), cell_cap + 1)
    spot_cells = jax.random.randint(spot_key, (domain_total,), 0, SIDE * SIDE)
    counts = jnp.where(local_cell == spot_cells[domain_of], cell_cap, counts)
    least_domain = (full_domain + 1 + jax.random.randint(least_key, (), 0, max(domain_total - 1, 1))) % domain_total
    least_spot = (domain_of == least_domain) & (local_cell == (spot_cells[domain_of] + 1) % (SIDE * SIDE))
    counts = jnp.where(least_spot, 1, counts)
    cell_keys = jax.random.split(order_key, LAT_Y * LAT_X)
    orders = jax.vmap(lambda one_key: jax.random.permutation(one_key, ENTRIES))(cell_keys)
    orders = orders.reshape(LAT_Y, LAT_X, ENTRIES).astype(jnp.int32)
    stencil_side = 2 * REACH + 1
    shift_y = orders // stencil_side - REACH
    shift_x = orders % stencil_side - REACH
    near_row = (lat_row[:, :, None] + shift_y) % LAT_Y
    near_col = (lat_col[:, :, None] + shift_x) % LAT_X
    cell_ids = near_row * LAT_X + near_col
    return (cell_ids.astype(jnp.int32), counts.astype(jnp.int32))


def draw_h_cols(key, part):
    return entry_lists(key, 11)[0]


def draw_h_count(key, part):
    return entry_lists(key, 11)[1]


def draw_z_cols(key, part):
    return entry_lists(key, 29)[0]


def draw_z_count(key, part):
    return entry_lists(key, 29)[1]


def steps_of(key, extent, shards, smallest, top_value):
    factor_of = 1.0
    for dim, parts in shards:
        draws = jax.random.uniform(jax.random.fold_in(jax.random.fold_in(key, 6), dim), (parts,), jnp.float32, smallest / len(shards), top_value / len(shards))
        factor_of = factor_of * jnp.repeat(jnp.exp(draws), extent[dim] // parts).reshape((-1,) + (1,) * (len(extent) - 1 - dim))
    return factor_of


def gaussian(own_key, extent, deviation, most, cuts=(), held_as=jnp.bfloat16):
    result = deviation * jax.random.normal(own_key, extent, jnp.float32)
    if cuts:
        result = result * steps_of(own_key, extent, cuts, -0.22, 0.18)
    return jnp.clip(result, -most, most).astype(held_as)


def setup_inputs(seed: int = 0) -> dict:
    key_list = jax.random.split(jax.random.key(seed), 8)
    return {
        "x_slab": draw_x_slab(jax.random.fold_in(key_list[7], 71), 0),
        "h_blocks": gaussian(key_list[1], (LAT_Y, LAT_X, ENTRIES, BLOCK * BLOCK), (ENTRIES * BLOCK // 2) ** -0.5, 0.21875, ((0, 4), (1, 8))),
        "h_cols": draw_h_cols(jax.random.fold_in(key_list[7], 71), 0),
        "h_count": draw_h_count(jax.random.fold_in(key_list[7], 71), 0),
        "z_blocks": gaussian(key_list[4], (LAT_Y, LAT_X, ENTRIES, BLOCK * BLOCK), (ENTRIES * BLOCK) ** -0.5, 0.15625, ((0, 4), (1, 8))),
        "z_cols": draw_z_cols(jax.random.fold_in(key_list[7], 71), 0),
        "z_count": draw_z_count(jax.random.fold_in(key_list[7], 71), 0),
    }


def apply_sparse(slab_field, blocks, col_ids, live_count):
    grid_rows, grid_cols, block_size, slab_cols = slab_field.shape
    max_entries = col_ids.shape[2]
    flat_grid = slab_field.reshape(grid_rows * grid_cols, block_size, slab_cols).astype(jnp.float32)
    is_live = (jnp.arange(max_entries, dtype=jnp.int32)[None, None, :] < live_count[:, :, None]).astype(jnp.float32)

    def one_row(packed):
        row_blocks, row_cols, row_live = packed
        picked = flat_grid[row_cols.astype(jnp.int32)] * row_live[:, :, None, None]
        block_mats = row_blocks.astype(jnp.float32).reshape(grid_cols, max_entries, block_size, block_size)
        return jnp.einsum('xkij,xkjs->xis', block_mats, picked)
    return lax.map(one_row, (blocks, col_ids, is_live))

def reference(x_slab, h_blocks, h_cols, h_count, z_blocks, z_cols, z_count):

    def apply_root(slab_field):
        return slab_field.astype(jnp.float32) + apply_sparse(slab_field, z_blocks, z_cols, z_count)

    def apply_hamilton(slab_field):
        return apply_sparse(slab_field, h_blocks, h_cols, h_count).astype(jnp.bfloat16)
    u_one = apply_root(x_slab).astype(jnp.bfloat16)
    u_two = apply_hamilton(u_one)
    power_image = apply_root(u_two)
    slab_float = x_slab.astype(jnp.float32)
    scale_ratio = jnp.sqrt(jnp.sum(power_image * power_image) / (jnp.sum(slab_float * slab_float) + 1e-06))
    cheb_one = (power_image / scale_ratio).astype(jnp.bfloat16)
    v_one = apply_root(cheb_one).astype(jnp.bfloat16)
    v_two = apply_hamilton(v_one)
    v_three = apply_root(v_two)
    cheb_two = (2.0 * v_three / scale_ratio - slab_float).astype(jnp.bfloat16)
    return (cheb_one, cheb_two)
```

```python
import functools

import jax
import jax.numpy as jnp
from jax import lax
from jax.experimental import pallas as pl
from jax.experimental.pallas import tpu as pltpu
from jax.sharding import PartitionSpec as P

MESH = pl.DeviceIdType.MESH
STEPS = 6
HALVES = 2
OWN = (0, 0)
FIRST = ((0, -1), (-1, -1), (1, -1), (-1, 0), (1, 0), (0, 1))
NEXT = (((-1, 0), (0, 1), (-1, 1)), ((1, 0), (0, 1), (1, 1)))
GROUPS = ((OWN,), ((-1, 0), (1, 0), (0, 1), (0, -1)), ((1, -1), (-1, -1)), ((-1, 1), (1, 1)))


def slot_of(alpha, beta):
    return (alpha + 1) * 3 + beta + 1


def kernel(rows, cols, side, block,
           x_ref, zb_hbm, zc_ref, zn_ref, hb_hbm, hc_ref, hn_ref,
           one_ref, two_ref,
           *scratch):
    bufs = [scratch[HALVES * step:HALVES * (step + 1)] for step in range(STEPS)]
    (z_raw, h_raw, spread, pair_tmp, z_wide, h_wide, power_ref, col_part, row_part,
     load_sem, send_sem, recv_sem, csend, crecv, rsend, rrecv) = scratch[HALVES * STEPS:]
    r = lax.axis_index("row")
    c = lax.axis_index("col")
    s = 1 - 2 * lax.rem(r, 2)
    t = 1 - 2 * lax.rem(c, 2)
    cells = side * side
    tall, width = x_ref.shape
    middle, halfway = tall // 2, width // 2
    slots = 9
    total = slots * cells
    pitch = spread.shape[0] // (block // 2)

    def at(alpha, beta):
        return (lax.rem(r + alpha * s + rows, rows), lax.rem(c + beta * t + cols, cols))

    z_load = pltpu.make_async_copy(zb_hbm, z_raw, load_sem.at[0])
    h_load = pltpu.make_async_copy(hb_hbm, h_raw, load_sem.at[1])
    z_load.start()
    h_load.start()

    barrier = pltpu.get_barrier_semaphore()
    greeted = 0
    for alpha in (-1, 0, 1):
        for beta in (-1, 0, 1):
            if alpha or beta:
                pl.semaphore_signal(barrier, inc=1, device_id=at(alpha, beta), device_id_type=MESH)
                greeted += 1
    for d in range(2, cols - 1):
        pl.semaphore_signal(barrier, inc=1, device_id=(r, lax.rem(c + d, cols)), device_id_type=MESH)
        greeted += 1
    for d in range(2, rows - 1):
        pl.semaphore_signal(barrier, inc=1, device_id=(lax.rem(r + d, rows), c), device_id_type=MESH)
        greeted += 1
    pl.semaphore_wait(barrier, greeted)

    def send(step, part, source, device, target):
        place = slot_of(*target)
        copy = pltpu.make_async_remote_copy(
            src_ref=bufs[step][part].at[slot_of(*source)],
            dst_ref=bufs[step][part].at[place],
            send_sem=send_sem.at[step, part, place],
            recv_sem=recv_sem.at[step, part, place],
            device_id=at(*device),
            device_id_type=MESH,
        )
        copy.start()
        return copy

    def begin(step, part):
        return {target: send(step, part, OWN, target, target) for target in FIRST}

    flying = {}
    landed = set()

    def arrive(step, part, where):
        if (step, part, where) not in landed:
            landed.add((step, part, where))
            flights = flying[step, part]
            flights[where].wait_recv()
            for source, device, target in NEXT:
                if source == where:
                    flights[target] = send(step, part, source, device, target)

    def finish(step, part, wide):
        buf = bufs[step][part]

        def product(where):
            slot = slot_of(*where)
            value = buf[slot]
            value = jnp.concatenate([value, pltpu.roll(value, halfway, 1)], axis=0)
            return jnp.dot(wide[slot], value, preferred_element_type=jnp.float32)

        acc = None
        for group in GROUPS:
            for where in group:
                if where != OWN:
                    arrive(step, part, where)
            for where in group:
                acc = product(where) if acc is None else acc + product(where)
        return acc

    def drain(flights):
        for copy in flights.values():
            copy.wait_send()

    def targets(width):
        place = lax.broadcasted_iota(jnp.int32, (pitch, width), 0)
        wanted = jnp.full((pitch, width), -1, jnp.int32)
        for alpha in (-1, 0, 1):
            for beta in (-1, 0, 1):
                row_at, col_at = at(alpha, beta)
                for cell in range(cells):
                    number = (row_at * side + cell // side) * (cols * side) + col_at * side + cell % side
                    wanted = jnp.where(place == slot_of(alpha, beta) * cells + cell, number, wanted)
        return wanted

    entries = z_raw.shape[1]
    area = z_raw.shape[2]
    half = block // 2
    pair = 2 * block
    wanted = targets(entries)
    entry = lax.broadcasted_iota(jnp.int32, (pitch, entries), 1)
    low = lax.broadcasted_iota(jnp.int32, (half, pair), 1) < block
    chunk = 4 * pair

    def arrange(raw, col_ref, count_ref, wide):
        for cell in range(cells):
            cy, cx = cell // side, cell % side
            named = col_ref[cy, cx:cx + 1, :]
            picked = (named == wanted) & (entry < count_ref[cy, cx])
            chooser = jnp.where(picked, 1.0, 0.0).astype(jnp.bfloat16)

            for part in range(area // chunk):
                got = jnp.dot(chooser, raw[cell, :, part * chunk:(part + 1) * chunk],
                              preferred_element_type=jnp.float32)
                for piece in range(chunk // pair):
                    line = part * (chunk // pair) + piece
                    spread[line * pitch:(line + 1) * pitch, :] = got[:, piece * pair:(piece + 1) * pair]

            def one_slot(slot, _):
                for duo in range(cells // 2):
                    first = spread[pl.ds(slot * cells + 2 * duo, half, stride=pitch), :]
                    second = spread[pl.ds(slot * cells + 2 * duo + 1, half, stride=pitch), :]
                    pair_tmp[duo, pl.ds(0, half, stride=2), :] = jnp.where(low, first, pltpu.roll(second, block, 1))
                    pair_tmp[duo, pl.ds(1, half, stride=2), :] = jnp.where(low, pltpu.roll(first, block, 1), second)
                for duo in range(cells // 2):
                    wide[slot, cell * block:(cell + 1) * block, duo * pair:(duo + 1) * pair] = (
                        pair_tmp[duo].astype(jnp.bfloat16))
                return 0

            lax.fori_loop(0, slots, one_slot, 0)

    left = lax.broadcasted_iota(jnp.int32, (middle, width), 1) < halfway
    own = slot_of(*OWN)

    def turn(value):
        return pltpu.roll(value, halfway, 1)

    def packed(value):
        top, low_rows = value[:middle], value[middle:]
        return (jnp.where(left, top, turn(low_rows)), jnp.where(left, turn(top), low_rows))

    def folded(value):
        return jnp.where(left, value[:middle], turn(value[middle:]))

    def unpacked(ref, parts):
        first, second = parts
        ref[:middle] = jnp.where(left, first, turn(second)).astype(ref.dtype)
        ref[middle:] = jnp.where(left, turn(first), second).astype(ref.dtype)

    both = range(HALVES)
    x_float = x_ref[...].astype(jnp.float32)
    for part, value in enumerate(packed(x_float)):
        bufs[0][part][own] = value.astype(jnp.bfloat16)
        flying[0, part] = begin(0, part)

    def advance(step, part, wide, root):
        value = folded(finish(step, part, wide))
        if root:
            value = bufs[step][part][own].astype(jnp.float32) + value
        if step + 1 < STEPS:
            bufs[step + 1][part][own] = value.astype(jnp.bfloat16)
            flying[step + 1, part] = begin(step + 1, part)
        return value

    z_load.wait()
    arrange(z_raw, zc_ref, zn_ref, z_wide)
    for part in both:
        advance(0, part, z_wide, True)
    h_load.wait()
    arrange(h_raw, hc_ref, hn_ref, h_wide)
    for part in both:
        advance(1, part, h_wide, False)
    x_square = jnp.sum(x_float * x_float, axis=0, keepdims=True)
    power_square = jnp.zeros((1, width), jnp.float32)
    for part in both:
        power = advance(2, part, z_wide, True)
        power_ref[part] = power
        power_square = power_square + jnp.sum(power * power, axis=0, keepdims=True)
    line_id = lax.broadcasted_iota(jnp.int32, col_part.shape[1:], 0)
    col_part[0] = jnp.where(line_id == 0, power_square, jnp.where(line_id == 1, x_square, 0.0))

    def gather_start(part, count, peer, ssem, rsem):
        copies = []
        for d in range(1, count):
            copy = pltpu.make_async_remote_copy(
                src_ref=part.at[0],
                dst_ref=part.at[d],
                send_sem=ssem.at[d],
                recv_sem=rsem.at[d],
                device_id=peer(d),
                device_id_type=MESH,
            )
            copy.start()
            copies.append(copy)
        return copies

    def gather_sum(part, copies):
        for copy in copies:
            copy.wait()
        return jnp.sum(part[...], axis=0)

    col_copies = gather_start(col_part, cols, lambda d: (r, lax.rem(c + d, cols)), csend, crecv)

    for part in both:
        advance(3, part, z_wide, True)
    row_part[0] = gather_sum(col_part, col_copies)
    row_copies = gather_start(row_part, rows, lambda d: (lax.rem(r + d, rows), c), rsend, rrecv)

    for part in both:
        advance(4, part, h_wide, False)
    sums = jnp.sum(gather_sum(row_part, row_copies), axis=1, keepdims=True)
    scale = jnp.sqrt(sums[0:1] / (sums[1:2] + 1e-06))
    inverse = 1.0 / scale
    unpacked(one_ref, [power_ref[part] / scale for part in both])
    for step in range(STEPS - 1):
        for part in both:
            drain(flying[step, part])

    x_parts = packed(x_float)
    ends = []
    for part in both:
        v_three = advance(5, part, z_wide, True)
        ends.append(2.0 * (v_three * inverse) * inverse - x_parts[part])
    unpacked(two_ref, ends)
    for part in both:
        drain(flying[5, part])


def solution(mesh):
    rows, cols = mesh.shape["row"], mesh.shape["col"]

    def body(x_slab, h_blocks, h_cols, h_count, z_blocks, z_cols, z_count):
        side, _, block, width = x_slab.shape
        entries, area = h_blocks.shape[2:]
        cells = side * side
        tall = cells * block
        pitch = -(-(9 * cells) // 8) * 8
        field = pltpu.VMEM((9, tall // HALVES, width), jnp.bfloat16)
        vmem = pl.BlockSpec(memory_space=pltpu.VMEM)
        smem = pl.BlockSpec(memory_space=pltpu.SMEM)
        hbm = pl.BlockSpec(memory_space=pl.ANY)
        out = jax.ShapeDtypeStruct((tall, width), jnp.bfloat16)
        one, two = pl.pallas_call(
            functools.partial(kernel, rows, cols, side, block),
            out_shape=(out, out),
            in_specs=[vmem, hbm, vmem, smem, hbm, vmem, smem],
            out_specs=(vmem, vmem),
            scratch_shapes=[field] * (STEPS * HALVES) + [
                pltpu.VMEM((cells, entries, area), jnp.bfloat16),
                pltpu.VMEM((cells, entries, area), jnp.bfloat16),
                pltpu.VMEM((block // 2 * pitch, 2 * block), jnp.float32),
                pltpu.VMEM((cells // 2, block, 2 * block), jnp.float32),
                pltpu.VMEM((9, tall, tall), jnp.bfloat16),
                pltpu.VMEM((9, tall, tall), jnp.bfloat16),
                pltpu.VMEM((HALVES, tall // HALVES, width), jnp.float32),
                pltpu.VMEM((cols, 8, width), jnp.float32),
                pltpu.VMEM((rows, 8, width), jnp.float32),
                pltpu.SemaphoreType.DMA((2,)),
                pltpu.SemaphoreType.DMA((STEPS, HALVES, 9)),
                pltpu.SemaphoreType.DMA((STEPS, HALVES, 9)),
                pltpu.SemaphoreType.DMA((cols,)),
                pltpu.SemaphoreType.DMA((cols,)),
                pltpu.SemaphoreType.DMA((rows,)),
                pltpu.SemaphoreType.DMA((rows,)),
            ],
            compiler_params=pltpu.CompilerParams(
                collective_id=0, has_side_effects=True, vmem_limit_bytes=40 * 1024 * 1024
            ),
            name="cheb",
        )(
            x_slab.reshape(tall, width),
            z_blocks.reshape(cells, entries, area), z_cols, z_count,
            h_blocks.reshape(cells, entries, area), h_cols, h_count,
        )
        return one.reshape(x_slab.shape), two.reshape(x_slab.shape)

    grid4 = P("row", "col", None, None)
    grid3 = P("row", "col", None)
    in_specs = (grid4, grid4, grid3, P("row", "col"), grid4, grid3, P("row", "col"))
    return jax.shard_map(body, mesh=mesh, in_specs=in_specs, out_specs=(grid4, grid4), check_vma=False)
```

```python
import functools

import jax
import jax.numpy as jnp
from jax import lax
from jax.experimental import pallas as pl
from jax.experimental.pallas import tpu as pltpu
from jax.sharding import PartitionSpec as P

MESH = pl.DeviceIdType.MESH
STEPS = 6
HALVES = 2
OWN = (0, 0)
FIRST = ((0, -1), (-1, -1), (1, -1), (-1, 0), (1, 0), (0, 1))
NEXT = (((-1, 0), (0, 1), (-1, 1)), ((1, 0), (0, 1), (1, 1)))
GROUPS = (((-1, 0), (1, 0), (0, 1), (0, -1), OWN), ((1, -1), (-1, -1), (-1, 1), (1, 1)))


def slot_of(alpha, beta):
    return (alpha + 1) * 3 + beta + 1


def kernel(rows, cols, side, block,
           x_ref, zb_hbm, zc_ref, zn_ref, hb_hbm, hc_ref, hn_ref,
           one_ref, two_ref,
           *scratch):
    bufs = [scratch[HALVES * step:HALVES * (step + 1)] for step in range(STEPS)]
    (z_raw, h_raw, spread, pair_tmp, z_wide, h_wide, power_ref, col_part, row_part,
     load_sem, send_sem, recv_sem, csend, crecv, rsend, rrecv) = scratch[HALVES * STEPS:]
    r = lax.axis_index("row")
    c = lax.axis_index("col")
    s = 1 - 2 * lax.rem(r, 2)
    t = 1 - 2 * lax.rem(c, 2)
    cells = side * side
    tall, width = x_ref.shape
    middle, halfway = tall // 2, width // 2
    slots = 9
    total = slots * cells
    pitch = spread.shape[0] // (block // 2)

    def at(alpha, beta):
        return (lax.rem(r + alpha * s + rows, rows), lax.rem(c + beta * t + cols, cols))

    z_load = pltpu.make_async_copy(zb_hbm, z_raw, load_sem.at[0])
    h_load = pltpu.make_async_copy(hb_hbm, h_raw, load_sem.at[1])
    z_load.start()
    h_load.start()

    barrier = pltpu.get_barrier_semaphore()
    greeted = 0
    for alpha in (-1, 0, 1):
        for beta in (-1, 0, 1):
            if alpha or beta:
                pl.semaphore_signal(barrier, inc=1, device_id=at(alpha, beta), device_id_type=MESH)
                greeted += 1
    for d in range(2, cols - 1):
        pl.semaphore_signal(barrier, inc=1, device_id=(r, lax.rem(c + d, cols)), device_id_type=MESH)
        greeted += 1
    for d in range(2, rows - 1):
        pl.semaphore_signal(barrier, inc=1, device_id=(lax.rem(r + d, rows), c), device_id_type=MESH)
        greeted += 1
    pl.semaphore_wait(barrier, greeted)

    def send(step, part, source, device, target):
        place = slot_of(*target)
        copy = pltpu.make_async_remote_copy(
            src_ref=bufs[step][part].at[slot_of(*source)],
            dst_ref=bufs[step][part].at[place],
            send_sem=send_sem.at[step, part, place],
            recv_sem=recv_sem.at[step, part, place],
            device_id=at(*device),
            device_id_type=MESH,
        )
        copy.start()
        return copy

    def begin(step, part):
        return {target: send(step, part, OWN, target, target) for target in FIRST}

    flying = {}
    landed = set()

    def arrive(step, part, where):
        if (step, part, where) not in landed:
            landed.add((step, part, where))
            flights = flying[step, part]
            flights[where].wait_recv()
            for source, device, target in NEXT:
                if source == where:
                    flights[target] = send(step, part, source, device, target)

    def relay(step, part):
        for source, _, _ in NEXT:
            arrive(step, part, source)

    def finish(step, part, wide):
        buf = bufs[step][part]

        def product(where):
            slot = slot_of(*where)
            value = buf[slot]
            value = jnp.concatenate([value, pltpu.roll(value, halfway, 1)], axis=0)
            return jnp.dot(wide[slot], value, preferred_element_type=jnp.float32)

        acc = None
        for group in GROUPS:
            for where in group:
                if where != OWN:
                    arrive(step, part, where)
            for where in group:
                acc = product(where) if acc is None else acc + product(where)
        return acc

    def drain(flights):
        for copy in flights.values():
            copy.wait_send()

    def targets(width):
        place = lax.broadcasted_iota(jnp.int32, (pitch, width), 0)
        wanted = jnp.full((pitch, width), -1, jnp.int32)
        for alpha in (-1, 0, 1):
            for beta in (-1, 0, 1):
                row_at, col_at = at(alpha, beta)
                for cell in range(cells):
                    number = (row_at * side + cell // side) * (cols * side) + col_at * side + cell % side
                    wanted = jnp.where(place == slot_of(alpha, beta) * cells + cell, number, wanted)
        return wanted

    entries = z_raw.shape[1]
    area = z_raw.shape[2]
    half = block // 2
    pair = 2 * block
    wanted = targets(entries)
    entry = lax.broadcasted_iota(jnp.int32, (pitch, entries), 1)
    low = lax.broadcasted_iota(jnp.int32, (half, pair), 1) < block
    chunk = 4 * pair

    def arrange(raw, col_ref, count_ref, wide, first, last):
        for cell in range(first, last):
            cy, cx = cell // side, cell % side
            named = col_ref[cy, cx:cx + 1, :]
            picked = (named == wanted) & (entry < count_ref[cy, cx])
            chooser = jnp.where(picked, 1.0, 0.0).astype(jnp.bfloat16)

            for part in range(area // chunk):
                got = jnp.dot(chooser, raw[cell, :, part * chunk:(part + 1) * chunk],
                              preferred_element_type=jnp.float32)
                for piece in range(chunk // pair):
                    line = part * (chunk // pair) + piece
                    spread[line * pitch:(line + 1) * pitch, :] = got[:, piece * pair:(piece + 1) * pair]

            def one_slot(slot, _):
                for duo in range(cells // 2):
                    first = spread[pl.ds(slot * cells + 2 * duo, half, stride=pitch), :]
                    second = spread[pl.ds(slot * cells + 2 * duo + 1, half, stride=pitch), :]
                    pair_tmp[duo, pl.ds(0, half, stride=2), :] = jnp.where(low, first, pltpu.roll(second, block, 1))
                    pair_tmp[duo, pl.ds(1, half, stride=2), :] = jnp.where(low, pltpu.roll(first, block, 1), second)
                for duo in range(cells // 2):
                    wide[slot, cell * block:(cell + 1) * block, duo * pair:(duo + 1) * pair] = (
                        pair_tmp[duo].astype(jnp.bfloat16))
                return 0

            lax.fori_loop(0, slots, one_slot, 0)

    left = lax.broadcasted_iota(jnp.int32, (middle, width), 1) < halfway
    own = slot_of(*OWN)

    def turn(value):
        return pltpu.roll(value, halfway, 1)

    def packed(value):
        top, low_rows = value[:middle], value[middle:]
        return (jnp.where(left, top, turn(low_rows)), jnp.where(left, turn(top), low_rows))

    def folded(value):
        return jnp.where(left, value[:middle], turn(value[middle:]))

    def unpacked(ref, parts):
        first, second = parts
        ref[:middle] = jnp.where(left, first, turn(second)).astype(ref.dtype)
        ref[middle:] = jnp.where(left, turn(first), second).astype(ref.dtype)

    both = range(HALVES)
    x_float = x_ref[...].astype(jnp.float32)
    for part, value in enumerate(packed(x_float)):
        bufs[0][part][own] = value.astype(jnp.bfloat16)
        flying[0, part] = begin(0, part)

    def advance(step, part, wide, root):
        value = folded(finish(step, part, wide))
        if root:
            value = bufs[step][part][own].astype(jnp.float32) + value
        if step + 1 < STEPS:
            bufs[step + 1][part][own] = value.astype(jnp.bfloat16)
            flying[step + 1, part] = begin(step + 1, part)
        return value

    z_load.wait()
    arrange(z_raw, zc_ref, zn_ref, z_wide, 0, cells)
    h_load.wait()
    early = cells // 4
    arrange(h_raw, hc_ref, hn_ref, h_wide, 0, early)
    relay(0, 0)
    arrange(h_raw, hc_ref, hn_ref, h_wide, early, 2 * early)
    advance(0, 0, z_wide, True)
    arrange(h_raw, hc_ref, hn_ref, h_wide, 2 * early, cells)
    advance(0, 1, z_wide, True)
    for part in both:
        advance(1, part, h_wide, False)
    x_square = jnp.sum(x_float * x_float, axis=0, keepdims=True)
    power_square = jnp.zeros((1, width), jnp.float32)
    for part in both:
        power = advance(2, part, z_wide, True)
        power_ref[part] = power
        power_square = power_square + jnp.sum(power * power, axis=0, keepdims=True)
    line_id = lax.broadcasted_iota(jnp.int32, col_part.shape[1:], 0)
    col_part[0] = jnp.where(line_id == 0, power_square, jnp.where(line_id == 1, x_square, 0.0))

    def gather_start(part, count, peer, ssem, rsem):
        copies = []
        for d in range(1, count):
            copy = pltpu.make_async_remote_copy(
                src_ref=part.at[0],
                dst_ref=part.at[d],
                send_sem=ssem.at[d],
                recv_sem=rsem.at[d],
                device_id=peer(d),
                device_id_type=MESH,
            )
            copy.start()
            copies.append(copy)
        return copies

    def gather_sum(part, copies):
        for copy in copies:
            copy.wait()
        return jnp.sum(part[...], axis=0)

    col_copies = gather_start(col_part, cols, lambda d: (r, lax.rem(c + d, cols)), csend, crecv)

    for part in both:
        advance(3, part, z_wide, True)
    row_part[0] = gather_sum(col_part, col_copies)
    row_copies = gather_start(row_part, rows, lambda d: (lax.rem(r + d, rows), c), rsend, rrecv)

    for part in both:
        advance(4, part, h_wide, False)
    sums = jnp.sum(gather_sum(row_part, row_copies), axis=1, keepdims=True)
    scale = jnp.sqrt(sums[0:1] / (sums[1:2] + 1e-06))
    inverse = 1.0 / scale
    unpacked(one_ref, [power_ref[part] / scale for part in both])
    x_parts = packed(x_float)
    ends = []
    for part in both:
        v_three = advance(5, part, z_wide, True)
        ends.append(2.0 * (v_three * inverse) * inverse - x_parts[part])
    unpacked(two_ref, ends)
    for flights in flying.values():
        drain(flights)


def solution(mesh):
    rows, cols = mesh.shape["row"], mesh.shape["col"]

    def body(x_slab, h_blocks, h_cols, h_count, z_blocks, z_cols, z_count):
        side, _, block, width = x_slab.shape
        entries, area = h_blocks.shape[2:]
        cells = side * side
        tall = cells * block
        pitch = -(-(9 * cells) // 8) * 8
        field = pltpu.VMEM((9, tall // HALVES, width), jnp.bfloat16)
        vmem = pl.BlockSpec(memory_space=pltpu.VMEM)
        smem = pl.BlockSpec(memory_space=pltpu.SMEM)
        hbm = pl.BlockSpec(memory_space=pl.ANY)
        out = jax.ShapeDtypeStruct((tall, width), jnp.bfloat16)
        one, two = pl.pallas_call(
            functools.partial(kernel, rows, cols, side, block),
            out_shape=(out, out),
            in_specs=[vmem, hbm, vmem, smem, hbm, vmem, smem],
            out_specs=(vmem, vmem),
            scratch_shapes=[field] * (STEPS * HALVES) + [
                pltpu.VMEM((cells, entries, area), jnp.bfloat16),
                pltpu.VMEM((cells, entries, area), jnp.bfloat16),
                pltpu.VMEM((block // 2 * pitch, 2 * block), jnp.float32),
                pltpu.VMEM((cells // 2, block, 2 * block), jnp.float32),
                pltpu.VMEM((9, tall, tall), jnp.bfloat16),
                pltpu.VMEM((9, tall, tall), jnp.bfloat16),
                pltpu.VMEM((HALVES, tall // HALVES, width), jnp.float32),
                pltpu.VMEM((cols, 8, width), jnp.float32),
                pltpu.VMEM((rows, 8, width), jnp.float32),
                pltpu.SemaphoreType.DMA((2,)),
                pltpu.SemaphoreType.DMA((STEPS, HALVES, 9)),
                pltpu.SemaphoreType.DMA((STEPS, HALVES, 9)),
                pltpu.SemaphoreType.DMA((cols,)),
                pltpu.SemaphoreType.DMA((cols,)),
                pltpu.SemaphoreType.DMA((rows,)),
                pltpu.SemaphoreType.DMA((rows,)),
            ],
            compiler_params=pltpu.CompilerParams(
                collective_id=0, has_side_effects=True, vmem_limit_bytes=40 * 1024 * 1024
            ),
            name="cheb",
        )(
            x_slab.reshape(tall, width),
            z_blocks.reshape(cells, entries, area), z_cols, z_count,
            h_blocks.reshape(cells, entries, area), h_cols, h_count,
        )
        return one.reshape(x_slab.shape), two.reshape(x_slab.shape)

    grid4 = P("row", "col", None, None)
    grid3 = P("row", "col", None)
    in_specs = (grid4, grid4, grid3, P("row", "col"), grid4, grid3, P("row", "col"))
    return jax.shard_map(body, mesh=mesh, in_specs=in_specs, out_specs=(grid4, grid4), check_vma=False)
```
